32 devices in a mesh: grp: 2 (over x), row: 8 (over z, y), col: 2 (over core).
Axes of the slice: x: 2, y: 2, z: 4, core: 2. Of those that a mesh axis runs over, the one named last changes fastest.
Arguments:
- upstream: float32 [1024, 384, 256], P(('grp', 'row'), 'col'), parts along dimension 0, may hold values from -6 to 6
- angle_codes: int32 [6, 2], P('grp'), parts along dimension 0, may hold values from 0 to 359
Outputs:
- downstream: float32 [1024, 384, 256], P('grp', 'row', 'col'), parts along dimension 0
The draws below stay inside these ranges and needn't reach their ends.
There are 2 independent parts, one for each index of `grp`. The reference program is written for one: setup_inputs(seed, part) draws one part's arguments, and reference() takes and returns one part's arrays. A program takes and returns all parts, laid end to end along the dimension named above; each array names one. Nothing has to cross between parts.
All inputs are finite; a program needn't handle non-finite values.
Results may differ from the reference program's by a relative error of at most 0.0003.
Values sent between devices are 32-bit elements; how exact they have to be, the bound alone decides.
No kernel may reach another device: no remote copies, remote signals or barrier semaphores. Data moves between devices by JAX's collectives and lax.ppermute only.
A program may use at most 128 MiB of HBM per device.

```python
import math
import jax
import jax.numpy as jnp

NX = 512
NY = 384
NZ = 256
ANGLES = 360
SHEARS = 3


def with_ends(drawn, stream_key, least, top_value):
    place = [jax.random.randint(jax.random.fold_in(stream_key, axis), (), 0, length) for axis, length in enumerate(drawn.shape)]
    widest = drawn.shape.index(max(drawn.shape))
    beside = place[:widest] + [(place[widest] + 1) % drawn.shape[widest]] + place[widest + 1:]
    return drawn.at[tuple(place)].set(least).at[tuple(beside)].set(top_value)


def block_scale(stream_key, extent, cuts, smallest, high):
    loudness, own = 1.0, jax.random.fold_in(stream_key, 6)
    for axis_at, shards_of in cuts:
        draws = jnp.exp(jax.random.uniform(jax.random.fold_in(own, axis_at), (shards_of,), jnp.float32, smallest / len(cuts), high / len(cuts)))
        loudness = loudness * jnp.repeat(draws, extent[axis_at] // shards_of).reshape([-1 if axis == axis_at else 1 for axis in range(len(extent))])
    return loudness


def normal_values(rng, extent, spread, most, shards=(), held_as=jnp.bfloat16):
    values = spread * jax.random.normal(rng, extent, jnp.float32)
    if shards:
        values = values * block_scale(rng, extent, shards, -0.22, 0.18)
    return jnp.clip(values, -most, most).astype(held_as)


def setup_inputs(seed: int = 0, part: int = 0) -> dict:
    arg_keys = jax.random.split(jax.random.key(seed), 3)
    own_keys = jax.random.split(jax.random.fold_in(arg_keys[2], part), 3)
    upstream = normal_values(own_keys[0], (NX, NY, NZ), 1.0, 6.0, ((0, 8), (1, 2)), jnp.float32)
    angle_codes = with_ends(jax.random.randint(own_keys[1], (SHEARS, 2), 0, ANGLES), jax.random.fold_in(own_keys[1], 1), 0, ANGLES - 1).astype(jnp.int32)
    return dict(upstream=upstream, angle_codes=angle_codes)


def shear_factors_of(angle_codes):
    return jnp.tan((angle_codes.astype(jnp.float32) - ANGLES / 2) * (math.pi / (2 * ANGLES)))


def shear_back(volume, along, offsets):
    length = volume.shape[along]
    position = jnp.arange(length, dtype=jnp.int32)
    frequency = jnp.where(position < length // 2, position, position - length).astype(jnp.float32)
    layout = [1, 1, 1]
    layout[along] = length
    phases = frequency.reshape(layout) * offsets * (2.0 * math.pi / length)
    ramp = jnp.cos(phases) + 1j * jnp.sin(phases)
    spectrum = jnp.fft.fft(volume, axis=along)
    return jnp.real(jnp.fft.ifft(spectrum * ramp, axis=along)).astype(jnp.float32)


def reference(upstream, angle_codes):
    factors = shear_factors_of(angle_codes)
    first_coords = jnp.arange(NX, dtype=jnp.float32) - NX / 2
    second_coords = jnp.arange(NY, dtype=jnp.float32) - NY / 2
    third_coords = jnp.arange(NZ, dtype=jnp.float32) - NZ / 2
    offsets = factors[2, 0] * first_coords[:, None, None] + factors[2, 1] * second_coords[None, :, None]
    after_third = shear_back(upstream, 2, offsets)
    offsets = factors[1, 0] * first_coords[:, None, None] + factors[1, 1] * third_coords[None, None, :]
    after_second = shear_back(after_third, 1, offsets)
    offsets = factors[0, 0] * second_coords[None, :, None] + factors[0, 1] * third_coords[None, None, :]
    return shear_back(after_second, 0, offsets)
```

```python
import functools
import math

import jax
import jax.numpy as jnp
import ml_dtypes
import numpy as np
from jax import lax
from jax.experimental import pallas as pl
from jax.experimental.pallas import tpu as pltpu
from jax.sharding import PartitionSpec as P

ANGLES = 360
F32 = jnp.float32
BF16 = jnp.bfloat16
VMEM_LIMIT = 58 * 1024 * 1024
XB = 4
HEAD = 2
CHUNKS = (3, 2, 1)
WINDOW = 5


def shear_factors_of(angle_codes):
    return jnp.tan((angle_codes.astype(F32) - ANGLES / 2) * (math.pi / (2 * ANGLES)))


def halves(matrix):
    high = matrix.astype(ml_dtypes.bfloat16)
    low = (matrix - high.astype(np.float64)).astype(ml_dtypes.bfloat16)
    return high, low


def direct_matrices(n):
    m = np.arange(n)
    f = np.arange(n // 2)
    theta = 2 * np.pi * ((m[:, None] * f[None, :]) % n) / n
    cosines, sines = np.cos(theta), np.sin(theta)
    sines[:, 0] = (-1.0) ** m
    weight = np.full(n // 2, 2.0 / n)
    weight[0] = 1.0 / n
    forward = np.concatenate([cosines, sines], 1)
    inverse = np.concatenate([cosines * weight, sines * weight], 1).T
    return forward, inverse


def split_matrices(n):
    half = n // 2
    m = np.arange(half)
    j = np.arange(half // 2)
    out = []
    for odd in (0, 1):
        theta = 2 * np.pi * (((2 * j + odd)[:, None] * m[None, :]) % n) / n
        cosines, sines = np.cos(theta), np.sin(theta)
        weight = np.full((half // 2, 1), 2.0 / n)
        if not odd:
            sines[0] = (-1.0) ** m
            weight[0] = 1.0 / n
        out.append(np.concatenate([cosines, sines], 0))
        out.append(np.concatenate([cosines * weight, sines * weight], 0).T)
    return out


def frequencies_split(n):
    j = np.arange(n // 4)
    even = 2 * j
    even[0] = n // 2
    return np.concatenate([even, 2 * j + 1]).astype(np.float32)


def lhs3(matrix):
    high, low = halves(matrix)
    return jnp.asarray(np.concatenate([high, high, low], 1))


def rhs3(matrix):
    high, low = halves(matrix)
    return jnp.asarray(np.concatenate([high, high, low], 0))


def split(value):
    high = value.astype(BF16)
    low = (value - high.astype(F32)).astype(BF16)
    return high, low


def turn(c, s, c1, s1, c2, s2, first):
    cp = c1 * c2 - s1 * s2
    sp = s1 * c2 + c1 * s2
    cpc = cp
    if first is not None:
        cpc = jnp.where(first, 1.0, cp)
        sp = jnp.where(first, 0.0, sp)
    return c * cpc + s * sp, s * cp - c * sp


def dot(a, b):
    return jnp.dot(a, b, preferred_element_type=F32)


def turns(frequency, offsets, n):
    u = frequency * offsets * (1.0 / n)
    p = (u - jnp.round(u)) * (2.0 * math.pi)
    return jnp.cos(p), jnp.sin(p)


def iota(shape, dim):
    return lax.broadcasted_iota(jnp.int32, shape, dim)


def third_kernel(x0, size, full, place, slopes, v_ref, fw_ref, iv_ref, own_ref, other_ref, c1_scr, s1_scr, c2_scr, s2_scr):
    xb, ny, n = v_ref.shape
    half = n // 2
    step = pl.program_id(0)

    @pl.when(step == 0)
    def _():
        def offsets(count, start, total, slope):
            return slope * ((iota((count, half), 0) + start).astype(F32) - total / 2)

        def frequency(count):
            f = iota((count, half), 1)
            return jnp.where(f == 0, half, f).astype(F32)

        padded = c1_scr.shape[0]
        c1_scr[...], s1_scr[...] = turns(
            frequency(padded), offsets(padded, place[1] + x0, full[0], slopes[4]), n
        )
        c2_scr[...], s2_scr[...] = turns(frequency(ny), offsets(ny, place[2] * ny, full[1], slopes[5]), n)

    v = v_ref[...].reshape(xb * ny, n)
    high, low = split(v)
    spectrum = dot(jnp.concatenate([high, low, high], 1), fw_ref[...])
    first = iota((ny, half), 1) == 0
    parts = []
    for x in range(xb):
        rows = slice(x * ny, (x + 1) * ny)
        at = pl.ds(step * xb + x, 1)
        c, s = turn(
            spectrum[rows, :half], spectrum[rows, half:],
            c1_scr[at, :], s1_scr[at, :], c2_scr[...], s2_scr[...], first,
        )
        parts.append(jnp.concatenate([c, s], 1))
    high, low = split(jnp.concatenate(parts, 0))
    back = dot(jnp.concatenate([high, low, high], 1), iv_ref[...])
    lower = back[:, :half].reshape(xb, ny, half)
    upper = back[:, half:].reshape(xb, ny, half)
    mine = place[2] == 0
    own_ref[...] = jnp.where(mine, lower, upper)
    other_ref[...] = jnp.where(mine, upper, lower)


def second_kernel(
    x0, heights, part, full, place, slopes, own_ref, other_ref, fe_ref, fo_ref, ie_ref, io_ref, *rest
):
    if heights:
        outs, (c1_scr, s1_scr, c2_scr, s2_scr, p_scr, q_scr) = rest[:-6], rest[-6:]
    else:
        (out,), (c1_scr, s1_scr, c2_scr, s2_scr) = rest[:-4], rest[-4:]
    xb, half, nk = own_ref.shape
    n = 2 * half
    quarter = half // 2
    blocks = half // part
    step = pl.program_id(0)

    @pl.when(step == 0)
    def _():
        def frequency(width):
            r = iota((half, width), 0)
            f = jnp.where(r < quarter, 2 * r, 2 * (r - quarter) + 1)
            return jnp.where(r == 0, half, f).astype(F32)

        lanes = iota((half, 128), 1)
        c1, s1 = turns(frequency(128), slopes[2] * ((lanes + (place[1] + x0)).astype(F32) - full[0] / 2), n)
        for b in range(c1_scr.shape[0]):
            c1_scr[b] = c1[:, b * xb : (b + 1) * xb]
            s1_scr[b] = s1[:, b * xb : (b + 1) * xb]
        lanes = iota((half, nk), 1)
        c2_scr[...], s2_scr[...] = turns(
            frequency(nk), slopes[3] * ((lanes + place[2] * nk).astype(F32) - full[2] / 2), n
        )

    col_sign = (1 - 2 * place[2]).astype(F32)
    row_sign = (1 - 2 * place[3]).astype(F32)
    first = iota((quarter, nk), 0) == 0
    for x0 in range(0, xb, 2):
        pair = (x0, x0 + 1)
        total = jnp.concatenate([own_ref[x] + other_ref[x] for x in pair], 1)
        delta = jnp.concatenate([own_ref[x] - other_ref[x] for x in pair], 1) * col_sign
        results = []
        for odd, (value, fw, iv) in enumerate(((total, fe_ref, ie_ref), (delta, fo_ref, io_ref))):
            high, low = split(value)
            spectrum = dot(fw[...], jnp.concatenate([high, low, high], 0))
            frows = slice(odd * quarter, (odd + 1) * quarter)
            c2, s2 = c2_scr[frows], s2_scr[frows]
            turned = []
            for k, x in enumerate(pair):
                lanes = slice(k * nk, (k + 1) * nk)
                c, s = turn(
                    spectrum[:quarter, lanes], spectrum[quarter:, lanes],
                    c1_scr[step, frows, x : x + 1], s1_scr[step, frows, x : x + 1], c2, s2,
                    None if odd else first,
                )
                turned.append(jnp.concatenate([c, s], 0))
            high, low = split(jnp.concatenate(turned, 1))
            results.append(dot(iv[...], jnp.concatenate([high, low, high], 0)))
        p, q = results
        if not heights:
            for base, value in ((0, p + q), (blocks, p - q)):
                for j in range(blocks):
                    for k, x in enumerate(pair):
                        out[base + j, x] = value[j * part : (j + 1) * part, k * nk : (k + 1) * nk]
            continue
        q = q * row_sign
        for j in range(blocks):
            p_scr[j] = p[j * part : (j + 1) * part]
            q_scr[j] = q[j * part : (j + 1) * part]
        for j in range(blocks):
            source = lax.bitwise_xor(place[0], j)
            p, q = p_scr[source], q_scr[source]
            for slot, value in ((j, p + q), (j + blocks, p - q)):
                y = 0
                for c, height in enumerate(heights):
                    for k, x in enumerate(pair):
                        outs[slot * len(heights) + c][x] = value[y : y + height, k * nk : (k + 1) * nk]
                    y += height


def first_kernel(place, slopes, head_ref, *refs):
    slots = head_ref.shape[0]
    blocks = slots // 2
    ins, rest = refs[:slots], refs[slots:]
    fe_ref, fo_ref, ie_ref, io_ref, c1_ref, s1_ref, c2_ref, s2_ref = rest[:8]
    out_ref, token_ref, e_scr, o_scr = rest[-4:]
    token_ref[...] = jnp.zeros_like(token_ref)
    n, ny, nk = out_ref.shape
    half, quarter = n // 2, n // 4
    heads, tails = head_ref.shape[1], ins[0].shape[0]
    row_sign = (1 - 2 * place[3]).astype(F32)
    first = iota((quarter, nk), 0) == 0
    aligned = ny % 8 == 0

    def flatten(ref):
        return ref.reshape(math.prod(ref.shape[:-1]), nk) if aligned else ref

    flat_head, flat, out_flat = flatten(head_ref), [flatten(ref) for ref in ins], flatten(out_ref)

    def head(side, y):
        if aligned:
            return flat_head[pl.ds(side * blocks * heads * ny + y, blocks * heads, stride=ny), :]
        return head_ref[side * blocks : (side + 1) * blocks, :, y, :].reshape(blocks * heads, nk)

    def column(slot, y):
        if aligned:
            return flat[slot][pl.ds(y, tails, stride=ny), :]
        return ins[slot][:, y, :]

    def keep(scr, at, count, value):
        high, low = split(value)
        for k, part in enumerate((high, low, high)):
            start = at + k * half
            if not isinstance(start, int):
                start = pl.multiple_of(start, 8)
            scr[pl.ds(start, count), :] = part

    for y0 in range(0, ny, 2):
        pair = (y0, y0 + 1)
        near = jnp.concatenate([head(0, y) for y in pair], 1)
        far = jnp.concatenate([head(1, y) for y in pair], 1)
        keep(e_scr, 0, blocks * heads, near + far)
        keep(o_scr, 0, blocks * heads, near - far)
        for j in range(blocks):
            at = lax.bitwise_xor(place[0], j) * tails + blocks * heads
            near = jnp.concatenate([column(j, y) for y in pair], 1)
            far = jnp.concatenate([column(j + blocks, y) for y in pair], 1)
            keep(e_scr, at, tails, near + far)
            keep(o_scr, at, tails, (near - far) * row_sign)
        results = []
        for odd, (scr, fw, iv) in enumerate(((e_scr, fe_ref, ie_ref), (o_scr, fo_ref, io_ref))):
            spectrum = dot(fw[...], scr[...])
            frows = slice(odd * quarter, (odd + 1) * quarter)
            c2, s2 = c2_ref[frows], s2_ref[frows]
            turned = []
            for k, y in enumerate(pair):
                lanes = slice(k * nk, (k + 1) * nk)
                c, s = turn(
                    spectrum[:quarter, lanes], spectrum[quarter:, lanes],
                    c1_ref[0, frows, y : y + 1], s1_ref[0, frows, y : y + 1], c2, s2,
                    None if odd else first,
                )
                turned.append(jnp.concatenate([c, s], 0))
            high, low = split(jnp.concatenate(turned, 1))
            results.append(dot(iv[...], jnp.concatenate([high, low, high], 0)))
        p, q = results
        for at, value in ((0, p + q), (half, p - q)):
            for k, y in enumerate(pair):
                column_out = value[:, k * nk : (k + 1) * nk]
                if aligned:
                    out_flat[pl.ds(at * ny + y, half, stride=ny), :] = column_out
                else:
                    out_ref[at : at + half, y, :] = column_out


def whole(array):
    rank = array.ndim
    return pl.BlockSpec(array.shape, lambda i, *_: (0,) * rank)


def call(kernel, grid, in_specs, out_specs, out_shape, scratch, flops, moved, aliases=None, name=None):
    return pl.pallas_call(
        kernel,
        out_shape=out_shape,
        grid_spec=pltpu.PrefetchScalarGridSpec(
            num_scalar_prefetch=2, grid=(grid,), in_specs=in_specs, out_specs=out_specs, scratch_shapes=scratch
        ),
        input_output_aliases=aliases or {},
        compiler_params=pltpu.CompilerParams(vmem_limit_bytes=VMEM_LIMIT),
        cost_estimate=pl.CostEstimate(flops=1, bytes_accessed=1, transcendentals=0),
        name=name,
    )


def body(upstream, angle_codes):
    factors = shear_factors_of(angle_codes)
    row_count, col_count = lax.axis_size("row"), lax.axis_size("col")
    row_place, col_place = lax.axis_index("row"), lax.axis_index("col")
    xl, yl, nz = upstream.shape
    nx, ny = xl * row_count, yl * col_count
    full = (nx, ny, nz)
    nk, part = nz // col_count, ny // row_count
    blocks = row_count // 2
    xb = XB
    head_x = xl * HEAD // 8 if xl >= 64 else xl // 2
    tail_x = xl - head_x
    heights = tuple(part * sixths // 6 for sixths in CHUNKS) if part % 48 == 0 else (part,)
    rows = 8 if part % 8 == 0 else part
    place = jnp.stack([row_place % blocks, row_place * xl, col_place, row_place // blocks]).astype(jnp.int32)
    slopes = factors.reshape(-1)

    z_forward, z_inverse = (rhs3(matrix) for matrix in direct_matrices(nz))
    y_mats = [lhs3(matrix) for matrix in split_matrices(ny)]
    y_mats = [y_mats[0], y_mats[2], y_mats[1], y_mats[3]]
    places = np.arange(nx // 2).reshape(blocks, xl)
    arrival = np.concatenate([places[:, :head_x].reshape(-1), places[:, head_x:].reshape(-1)])
    x_even, x_even_back, x_odd, x_odd_back = split_matrices(nx)
    x_mats = [lhs3(matrix) for matrix in (x_even[:, arrival], x_odd[:, arrival], x_even_back, x_odd_back)]

    def third(x0, size, volume):
        base = x0 // xb
        out = pl.BlockSpec((xb, yl, nk), lambda i, *_: (i, 0, 0))
        near = pltpu.VMEM((-(-size // 8) * 8, nz // 2), F32)
        far = pltpu.VMEM((yl, nz // 2), F32)
        return call(
            functools.partial(third_kernel, x0, size, full), size // xb,
            [pl.BlockSpec((xb, yl, nz), lambda i, *_: (base + i, 0, 0)), whole(z_forward), whole(z_inverse)],
            [out, out],
            [jax.ShapeDtypeStruct((size, yl, nk), F32)] * 2,
            [near, near, far, far], 12 * size * yl * nz * nz, 8 * size * yl * nz, name="third",
        )(place, slopes, volume, z_forward, z_inverse)

    def second(x0, size, own, other, heights):
        data = pl.BlockSpec((xb, yl, nk), lambda i, *_: (i, 0, 0))
        near = pltpu.VMEM((size // xb, ny // 2, xb), F32)
        far = pltpu.VMEM((ny // 2, nk), F32)
        scratch = [near, near, far, far]
        if heights:
            scratch += [pltpu.VMEM((blocks, part, 2 * nk), F32)] * 2
            specs = [pl.BlockSpec((xb, height, nk), lambda i, *_: (i, 0, 0)) for height in heights] * row_count
            shapes = [jax.ShapeDtypeStruct((size, height, nk), F32) for height in heights] * row_count
        else:
            specs = [pl.BlockSpec((row_count, xb, part, nk), lambda i, *_: (0, i, 0, 0))]
            shapes = [jax.ShapeDtypeStruct((row_count, size, part, nk), F32)]
        return call(
            functools.partial(second_kernel, x0, heights, part, full), size // xb,
            [data, data] + [whole(matrix) for matrix in y_mats],
            specs, shapes, scratch, 6 * size * ny * nk * ny, 8 * size * ny * nk, name="second",
        )(place, slopes, own, other, *y_mats)

    sent = []
    order = [d for pair in zip(range(blocks, row_count), range(blocks)) for d in pair if d]

    def after(value, *others):
        return lax.optimization_barrier((value, *others))[0]

    def spread(pieces, gates=None):
        got = [pieces[0]] + [None] * (row_count - 1)
        for i, d in enumerate(order):
            others = list(sent[-WINDOW:][:1]) if len(sent) >= WINDOW else []
            if gates and i in gates:
                others.append(gates[i])
            got[d] = lax.ppermute(after(pieces[d], *others), "row", [(i, i ^ d) for i in range(row_count)])
            sent.append(got[d])
        return got

    swap = [(0, 1), (1, 0)]
    own, other = third(0, head_x, upstream)
    (head,) = second(0, head_x, own, lax.ppermute(other, "col", swap), None)
    volume = after(upstream, head)
    head = lax.all_to_all(head, "row", 0, 0, tiled=True)
    own, other = third(head_x, tail_x, volume)
    outs = second(head_x, tail_x, own, lax.ppermute(other, "col", swap), heights)
    pieces = [[outs[d * len(heights) + c] for d in range(row_count)] for c in range(len(heights))]

    def waves(frequency, offsets, n):
        p = frequency * offsets * (2.0 * math.pi / n)
        return jnp.cos(p), jnp.sin(p)

    def centred(length, start, total):
        return (lax.iota(jnp.int32, length) + start).astype(F32) - total / 2

    late = after(slopes, outs[0])
    fx = frequencies_split(nx)
    xc1, xs1 = waves(fx[None, :, None], (late[0] * centred(part, row_place * part, ny)).reshape(-1, 1, rows), nx)
    xc2, xs2 = waves(fx[:, None], (late[1] * centred(nk, col_place * nk, nz))[None, :], nx)

    def first(y0, height, got, result, token):
        base = y0 // rows
        ins = [head, *got]
        specs = [pl.BlockSpec((row_count, head_x, rows, nk), lambda i, *_: (0, 0, base + i, 0))]
        specs += [pl.BlockSpec((tail_x, rows, nk), lambda i, *_: (0, i, 0))] * row_count
        table = pl.BlockSpec((1, nx // 2, rows), lambda i, *_: (base + i, 0, 0))
        ins += [*x_mats, xc1, xs1, xc2, xs2]
        specs += [whole(matrix) for matrix in x_mats] + [table, table, whole(xc2), whole(xs2)]
        aliases = {}
        if result is not None:
            aliases = {len(ins) + 2: 0}
            ins += [result, token]
            specs += [pl.BlockSpec(memory_space=pl.ANY)] * 2
        scratch = pltpu.VMEM((3 * nx // 2, 2 * nk), BF16)
        return call(
            first_kernel, height // rows,
            specs,
            [pl.BlockSpec((nx, rows, nk), lambda i, *_: (0, base + i, 0)), pl.BlockSpec((8, 128), lambda i, *_: (0, 0))],
            [jax.ShapeDtypeStruct((nx, part, nk), F32), jax.ShapeDtypeStruct((8, 128), F32)],
            [scratch, scratch], 6 * nx * height * nk * nx, 8 * nx * height * nk, aliases, name="first",
        )(place, slopes, *ins)

    result, token, tokens, y0 = None, None, [], 0
    got = [spread(pieces[0], {i: head for i in range(WINDOW)})]
    for c, height in enumerate(heights):
        ahead = c + 1
        if ahead < len(heights):
            gates = {}
            if c >= 1:
                gates[0] = tokens[c - 1]
            if ahead == len(heights) - 1 and c >= 1:
                result, token = first(y0, height, got[c], result, token)
                tokens.append(token)
                gates[len(order) - 2] = token
            got.append(spread(pieces[ahead], gates))
        if len(tokens) == c:
            result, token = first(y0, height, got[c], result, token)
            tokens.append(token)
        y0 += height
    return result


def solution(mesh):
    placed = (P(("grp", "row"), "col", None), P("grp", None))
    return jax.shard_map(
        body, mesh=mesh, in_specs=placed, out_specs=P("grp", "row", "col"), check_vma=False
    )
```

```python
import functools
import math

import jax
import jax.numpy as jnp
import ml_dtypes
import numpy as np
from jax import lax
from jax.experimental import pallas as pl
from jax.experimental.pallas import tpu as pltpu
from jax.sharding import PartitionSpec as P

ANGLES = 360
F32 = jnp.float32
BF16 = jnp.bfloat16
VMEM_LIMIT = 58 * 1024 * 1024
XB = 8
HEAD = 2
CHUNKS = (3, 2, 1)
GATES = (2,)
WINDOW = 5


def shear_factors_of(angle_codes):
    return jnp.tan((angle_codes.astype(F32) - ANGLES / 2) * (math.pi / (2 * ANGLES)))


def halves(matrix):
    high = matrix.astype(ml_dtypes.bfloat16)
    low = (matrix - high.astype(np.float64)).astype(ml_dtypes.bfloat16)
    return high, low


def direct_matrices(n):
    m = np.arange(n)
    f = np.arange(n // 2)
    theta = 2 * np.pi * ((m[:, None] * f[None, :]) % n) / n
    cosines, sines = np.cos(theta), np.sin(theta)
    sines[:, 0] = (-1.0) ** m
    weight = np.full(n // 2, 2.0 / n)
    weight[0] = 1.0 / n
    forward = np.concatenate([cosines, sines], 1)
    inverse = np.concatenate([cosines * weight, sines * weight], 1).T
    return forward, inverse


def split_matrices(n):
    half = n // 2
    m = np.arange(half)
    j = np.arange(half // 2)
    out = []
    for odd in (0, 1):
        theta = 2 * np.pi * (((2 * j + odd)[:, None] * m[None, :]) % n) / n
        cosines, sines = np.cos(theta), np.sin(theta)
        weight = np.full((half // 2, 1), 2.0 / n)
        if not odd:
            sines[0] = (-1.0) ** m
            weight[0] = 1.0 / n
        out.append(np.concatenate([cosines, sines], 0))
        out.append(np.concatenate([cosines * weight, sines * weight], 0).T)
    return out


def frequencies_split(n):
    j = np.arange(n // 4)
    even = 2 * j
    even[0] = n // 2
    return np.concatenate([even, 2 * j + 1]).astype(np.float32)


def lhs3(matrix):
    high, low = halves(matrix)
    return jnp.asarray(np.concatenate([high, high, low], 1))


def rhs3(matrix):
    high, low = halves(matrix)
    return jnp.asarray(np.concatenate([high, high, low], 0))


def split(value):
    high = value.astype(BF16)
    low = (value - high.astype(F32)).astype(BF16)
    return high, low


def turn(c, s, c1, s1, c2, s2, first):
    cp = c1 * c2 - s1 * s2
    sp = s1 * c2 + c1 * s2
    cpc = cp
    if first is not None:
        cpc = jnp.where(first, 1.0, cp)
        sp = jnp.where(first, 0.0, sp)
    return c * cpc + s * sp, s * cp - c * sp


def dot(a, b):
    return jnp.dot(a, b, preferred_element_type=F32)


def turns(frequency, offsets, n):
    u = frequency * offsets * (1.0 / n)
    p = (u - jnp.round(u)) * (2.0 * math.pi)
    return jnp.cos(p), jnp.sin(p)


def iota(shape, dim):
    return lax.broadcasted_iota(jnp.int32, shape, dim)


def third_kernel(x0, size, full, place, slopes, v_ref, fw_ref, iv_ref, own_ref, other_ref, c1_scr, s1_scr, c2_scr, s2_scr):
    xb, ny, n = v_ref.shape
    half = n // 2
    step = pl.program_id(0)

    @pl.when(step == 0)
    def _():
        def offsets(count, start, total, slope):
            return slope * ((iota((count, half), 0) + start).astype(F32) - total / 2)

        def frequency(count):
            f = iota((count, half), 1)
            return jnp.where(f == 0, half, f).astype(F32)

        padded = c1_scr.shape[0]
        c1_scr[...], s1_scr[...] = turns(
            frequency(padded), offsets(padded, place[1] + x0, full[0], slopes[2, 0]), n
        )
        c2_scr[...], s2_scr[...] = turns(frequency(ny), offsets(ny, place[2] * ny, full[1], slopes[2, 1]), n)

    first = iota((ny, half), 1) == 0
    mine = place[2] == 0
    for x in range(xb):
        high, low = split(v_ref[x])
        spectrum = dot(jnp.concatenate([high, low, high], 1), fw_ref[...])
        at = pl.ds(step * xb + x, 1)
        c, s = turn(
            spectrum[:, :half], spectrum[:, half:], c1_scr[at, :], s1_scr[at, :], c2_scr[...], s2_scr[...], first
        )
        high, low = split(jnp.concatenate([c, s], 1))
        back = dot(jnp.concatenate([high, low, high], 1), iv_ref[...])
        lower, upper = back[:, :half], back[:, half:]
        own_ref[x] = jnp.where(mine, lower, upper)
        other_ref[x] = jnp.where(mine, upper, lower)


def second_kernel(
    x0, heights, part, full, place, slopes, own_ref, other_ref, fe_ref, fo_ref, ie_ref, io_ref, *rest
):
    if heights:
        outs, (c1_scr, s1_scr, c2_scr, s2_scr, p_scr, q_scr) = rest[:-6], rest[-6:]
    else:
        (out,), (c1_scr, s1_scr, c2_scr, s2_scr) = rest[:-4], rest[-4:]
    xb, half, nk = own_ref.shape
    n = 2 * half
    quarter = half // 2
    blocks = half // part
    step = pl.program_id(0)

    @pl.when(step == 0)
    def _():
        def frequency(width):
            r = iota((half, width), 0)
            f = jnp.where(r < quarter, 2 * r, 2 * (r - quarter) + 1)
            return jnp.where(r == 0, half, f).astype(F32)

        lanes = iota((half, 128), 1)
        c1, s1 = turns(frequency(128), slopes[1, 0] * ((lanes + (place[1] + x0)).astype(F32) - full[0] / 2), n)
        for b in range(c1_scr.shape[0]):
            c1_scr[b] = c1[:, b * xb : (b + 1) * xb]
            s1_scr[b] = s1[:, b * xb : (b + 1) * xb]
        lanes = iota((half, nk), 1)
        c2_scr[...], s2_scr[...] = turns(
            frequency(nk), slopes[1, 1] * ((lanes + place[2] * nk).astype(F32) - full[2] / 2), n
        )

    col_sign = (1 - 2 * place[2]).astype(F32)
    row_sign = (1 - 2 * place[3]).astype(F32)
    first = iota((quarter, nk), 0) == 0
    for x0 in range(0, xb, 2):
        pair = (x0, x0 + 1)
        total = jnp.concatenate([own_ref[x] + other_ref[x] for x in pair], 1)
        delta = jnp.concatenate([own_ref[x] - other_ref[x] for x in pair], 1) * col_sign
        results = []
        for odd, (value, fw, iv) in enumerate(((total, fe_ref, ie_ref), (delta, fo_ref, io_ref))):
            high, low = split(value)
            spectrum = dot(fw[...], jnp.concatenate([high, low, high], 0))
            frows = slice(odd * quarter, (odd + 1) * quarter)
            c2, s2 = c2_scr[frows], s2_scr[frows]
            turned = []
            for k, x in enumerate(pair):
                lanes = slice(k * nk, (k + 1) * nk)
                c, s = turn(
                    spectrum[:quarter, lanes], spectrum[quarter:, lanes],
                    c1_scr[step, frows, x : x + 1], s1_scr[step, frows, x : x + 1], c2, s2,
                    None if odd else first,
                )
                turned.append(jnp.concatenate([c, s], 0))
            high, low = split(jnp.concatenate(turned, 1))
            results.append(dot(iv[...], jnp.concatenate([high, low, high], 0)))
        p, q = results
        if not heights:
            for base, value in ((0, p + q), (blocks, p - q)):
                for j in range(blocks):
                    for k, x in enumerate(pair):
                        out[base + j, x] = value[j * part : (j + 1) * part, k * nk : (k + 1) * nk]
            continue
        q = q * row_sign
        for j in range(blocks):
            p_scr[j] = p[j * part : (j + 1) * part]
            q_scr[j] = q[j * part : (j + 1) * part]
        for j in range(blocks):
            source = lax.bitwise_xor(place[0], j)
            p, q = p_scr[source], q_scr[source]
            for slot, value in ((j, p + q), (j + blocks, p - q)):
                y = 0
                for c, height in enumerate(heights):
                    for k, x in enumerate(pair):
                        outs[slot * len(heights) + c][x] = value[y : y + height, k * nk : (k + 1) * nk]
                    y += height


def first_kernel(place, slopes, head_ref, *refs):
    slots = head_ref.shape[0]
    blocks = slots // 2
    ins, rest = refs[:slots], refs[slots:]
    fe_ref, fo_ref, ie_ref, io_ref, c1_ref, s1_ref, c2_ref, s2_ref = rest[:8]
    out_ref, token_ref, e_scr, o_scr = rest[-4:]
    token_ref[...] = jnp.zeros_like(token_ref)
    n, ny, nk = out_ref.shape
    half, quarter = n // 2, n // 4
    heads, tails = head_ref.shape[1], ins[0].shape[0]
    row_sign = (1 - 2 * place[3]).astype(F32)
    first = iota((quarter, nk), 0) == 0
    aligned = ny % 8 == 0

    def flatten(ref):
        return ref.reshape(math.prod(ref.shape[:-1]), nk) if aligned else ref

    flat_head, flat, out_flat = flatten(head_ref), [flatten(ref) for ref in ins], flatten(out_ref)

    def head(side, y):
        if aligned:
            return flat_head[pl.ds(side * blocks * heads * ny + y, blocks * heads, stride=ny), :]
        return head_ref[side * blocks : (side + 1) * blocks, :, y, :].reshape(blocks * heads, nk)

    def column(slot, y):
        if aligned:
            return flat[slot][pl.ds(y, tails, stride=ny), :]
        return ins[slot][:, y, :]

    def keep(scr, at, count, value):
        high, low = split(value)
        for k, part in enumerate((high, low, high)):
            start = at + k * half
            if not isinstance(start, int):
                start = pl.multiple_of(start, 8)
            scr[pl.ds(start, count), :] = part

    for y0 in range(0, ny, 2):
        pair = (y0, y0 + 1)
        near = jnp.concatenate([head(0, y) for y in pair], 1)
        far = jnp.concatenate([head(1, y) for y in pair], 1)
        keep(e_scr, 0, blocks * heads, near + far)
        keep(o_scr, 0, blocks * heads, near - far)
        for j in range(blocks):
            at = lax.bitwise_xor(place[0], j) * tails + blocks * heads
            near = jnp.concatenate([column(j, y) for y in pair], 1)
            far = jnp.concatenate([column(j + blocks, y) for y in pair], 1)
            keep(e_scr, at, tails, near + far)
            keep(o_scr, at, tails, (near - far) * row_sign)
        results = []
        for odd, (scr, fw, iv) in enumerate(((e_scr, fe_ref, ie_ref), (o_scr, fo_ref, io_ref))):
            spectrum = dot(fw[...], scr[...])
            frows = slice(odd * quarter, (odd + 1) * quarter)
            c2, s2 = c2_ref[frows], s2_ref[frows]
            turned = []
            for k, y in enumerate(pair):
                lanes = slice(k * nk, (k + 1) * nk)
                c, s = turn(
                    spectrum[:quarter, lanes], spectrum[quarter:, lanes],
                    c1_ref[0, frows, y : y + 1], s1_ref[0, frows, y : y + 1], c2, s2,
                    None if odd else first,
                )
                turned.append(jnp.concatenate([c, s], 0))
            high, low = split(jnp.concatenate(turned, 1))
            results.append(dot(iv[...], jnp.concatenate([high, low, high], 0)))
        p, q = results
        for at, value in ((0, p + q), (half, p - q)):
            for k, y in enumerate(pair):
                column_out = value[:, k * nk : (k + 1) * nk]
                if aligned:
                    out_flat[pl.ds(at * ny + y, half, stride=ny), :] = column_out
                else:
                    out_ref[at : at + half, y, :] = column_out


def whole(array):
    rank = array.ndim
    return pl.BlockSpec(array.shape, lambda i, *_: (0,) * rank)


def call(kernel, grid, in_specs, out_specs, out_shape, scratch, flops, moved, aliases=None, name=None):
    return pl.pallas_call(
        kernel,
        out_shape=out_shape,
        grid_spec=pltpu.PrefetchScalarGridSpec(
            num_scalar_prefetch=2, grid=(grid,), in_specs=in_specs, out_specs=out_specs, scratch_shapes=scratch
        ),
        input_output_aliases=aliases or {},
        compiler_params=pltpu.CompilerParams(vmem_limit_bytes=VMEM_LIMIT),
        cost_estimate=pl.CostEstimate(flops=1, bytes_accessed=1, transcendentals=0),
        name=name,
    )


def body(upstream, angle_codes):
    factors = shear_factors_of(angle_codes)
    row_count, col_count = lax.axis_size("row"), lax.axis_size("col")
    row_place, col_place = lax.axis_index("row"), lax.axis_index("col")
    xl, yl, nz = upstream.shape
    nx, ny = xl * row_count, yl * col_count
    full = (nx, ny, nz)
    nk, part = nz // col_count, ny // row_count
    blocks = row_count // 2
    xb = XB
    head_x = xl * HEAD // 8 if xl >= 64 else xl // 2
    tail_x = xl - head_x
    heights = tuple(part * sixths // 6 for sixths in CHUNKS) if part % 48 == 0 else (part,)
    rows = 8 if part % 8 == 0 else part
    place = jnp.stack([row_place % blocks, row_place * xl, col_place, row_place // blocks]).astype(jnp.int32)
    slopes = factors

    z_forward, z_inverse = (rhs3(matrix) for matrix in direct_matrices(nz))
    y_mats = [lhs3(matrix) for matrix in split_matrices(ny)]
    y_mats = [y_mats[0], y_mats[2], y_mats[1], y_mats[3]]
    places = np.arange(nx // 2).reshape(blocks, xl)
    arrival = np.concatenate([places[:, :head_x].reshape(-1), places[:, head_x:].reshape(-1)])
    x_even, x_even_back, x_odd, x_odd_back = split_matrices(nx)
    x_mats = [lhs3(matrix) for matrix in (x_even[:, arrival], x_odd[:, arrival], x_even_back, x_odd_back)]

    def third(x0, size, volume):
        base = x0 // xb
        out = pl.BlockSpec((xb, yl, nk), lambda i, *_: (i, 0, 0))
        near = pltpu.VMEM((-(-size // 8) * 8, nz // 2), F32)
        far = pltpu.VMEM((yl, nz // 2), F32)
        return call(
            functools.partial(third_kernel, x0, size, full), size // xb,
            [pl.BlockSpec((xb, yl, nz), lambda i, *_: (base + i, 0, 0)), whole(z_forward), whole(z_inverse)],
            [out, out],
            [jax.ShapeDtypeStruct((size, yl, nk), F32)] * 2,
            [near, near, far, far], 12 * size * yl * nz * nz, 8 * size * yl * nz, name="third",
        )(place, slopes, volume, z_forward, z_inverse)

    def second(x0, size, own, other, heights):
        data = pl.BlockSpec((xb, yl, nk), lambda i, *_: (i, 0, 0))
        near = pltpu.VMEM((size // xb, ny // 2, xb), F32)
        far = pltpu.VMEM((ny // 2, nk), F32)
        scratch = [near, near, far, far]
        if heights:
            scratch += [pltpu.VMEM((blocks, part, 2 * nk), F32)] * 2
            specs = [pl.BlockSpec((xb, height, nk), lambda i, *_: (i, 0, 0)) for height in heights] * row_count
            shapes = [jax.ShapeDtypeStruct((size, height, nk), F32) for height in heights] * row_count
        else:
            specs = [pl.BlockSpec((row_count, xb, part, nk), lambda i, *_: (0, i, 0, 0))]
            shapes = [jax.ShapeDtypeStruct((row_count, size, part, nk), F32)]
        return call(
            functools.partial(second_kernel, x0, heights, part, full), size // xb,
            [data, data] + [whole(matrix) for matrix in y_mats],
            specs, shapes, scratch, 6 * size * ny * nk * ny, 8 * size * ny * nk, name="second",
        )(place, slopes, own, other, *y_mats)

    sent = []
    order = [d for pair in zip([*range(1, blocks), 0], range(blocks, row_count)) for d in pair if d]

    def after(value, *others):
        return lax.optimization_barrier((value, *others))[0]

    def spread(pieces, gates=None):
        got = [pieces[0]] + [None] * (row_count - 1)
        for i, d in enumerate(order):
            others = list(sent[-WINDOW:][:1]) if len(sent) >= WINDOW else []
            if gates and i in gates:
                others.append(gates[i])
            got[d] = lax.ppermute(after(pieces[d], *others), "row", [(i, i ^ d) for i in range(row_count)])
            sent.append(got[d])
        return got

    swap = [(0, 1), (1, 0)]
    own, other = third(0, head_x, upstream)
    (head,) = second(0, head_x, own, lax.ppermute(other, "col", swap), None)
    volume = after(upstream, head)
    head = lax.all_to_all(head, "row", 0, 0, tiled=True)
    own, other = third(head_x, tail_x, volume)
    outs = second(head_x, tail_x, own, lax.ppermute(other, "col", swap), heights)
    pieces = [[outs[d * len(heights) + c] for d in range(row_count)] for c in range(len(heights))]

    def waves(frequency, offsets, n):
        p = frequency * offsets * (2.0 * math.pi / n)
        return jnp.cos(p), jnp.sin(p)

    def centred(length, start, total):
        return (lax.iota(jnp.int32, length) + start).astype(F32) - total / 2

    late = after(slopes, outs[0])
    fx = frequencies_split(nx)
    xc1, xs1 = waves(fx[None, :, None], (late[0, 0] * centred(part, row_place * part, ny)).reshape(-1, 1, rows), nx)
    xc2, xs2 = waves(fx[:, None], (late[0, 1] * centred(nk, col_place * nk, nz))[None, :], nx)

    def first(y0, height, got, result, token):
        base = y0 // rows
        ins = [head, *got]
        specs = [pl.BlockSpec((row_count, head_x, rows, nk), lambda i, *_: (0, 0, base + i, 0))]
        specs += [pl.BlockSpec((tail_x, rows, nk), lambda i, *_: (0, i, 0))] * row_count
        table = pl.BlockSpec((1, nx // 2, rows), lambda i, *_: (base + i, 0, 0))
        ins += [*x_mats, xc1, xs1, xc2, xs2]
        specs += [whole(matrix) for matrix in x_mats] + [table, table, whole(xc2), whole(xs2)]
        aliases = {}
        if result is not None:
            aliases = {len(ins) + 2: 0}
            ins += [result, token]
            specs += [pl.BlockSpec(memory_space=pl.ANY)] * 2
        scratch = pltpu.VMEM((3 * nx // 2, 2 * nk), BF16)
        return call(
            first_kernel, height // rows,
            specs,
            [pl.BlockSpec((nx, rows, nk), lambda i, *_: (0, base + i, 0)), pl.BlockSpec((8, 128), lambda i, *_: (0, 0))],
            [jax.ShapeDtypeStruct((nx, part, nk), F32), jax.ShapeDtypeStruct((8, 128), F32)],
            [scratch, scratch], 6 * nx * height * nk * nx, 8 * nx * height * nk, aliases, name="first",
        )(place, slopes, *ins)

    result, token, tokens, y0 = None, None, [], 0
    got = [spread(pieces[0], {i: head for i in GATES})]
    for c, height in enumerate(heights):
        ahead = c + 1
        if ahead < len(heights):
            gates = {}
            if c >= 1:
                gates[0] = tokens[c - 1]
            if ahead == len(heights) - 1 and c >= 1:
                result, token = first(y0, height, got[c], result, token)
                tokens.append(token)
                gates[len(order) - 2] = token
            got.append(spread(pieces[ahead], gates))
        if len(tokens) == c:
            result, token = first(y0, height, got[c], result, token)
            tokens.append(token)
        y0 += height
    return result


def solution(mesh):
    placed = (P(("grp", "row"), "col", None), P("grp", None))
    return jax.shard_map(
        body, mesh=mesh, in_specs=placed, out_specs=P("grp", "row", "col"), check_vma=False
    )
```

```python
import functools
import math

import jax
import jax.numpy as jnp
import ml_dtypes
import numpy as np
from jax import lax
from jax.experimental import pallas as pl
from jax.experimental.pallas import tpu as pltpu
from jax.sharding import PartitionSpec as P

ANGLES = 360
F32 = jnp.float32
BF16 = jnp.bfloat16
VMEM_LIMIT = 58 * 1024 * 1024
XB = 8
HEAD = 2
CHUNKS = (3, 2, 1)
GATES = (2,)
WINDOW = 5


def shear_factors_of(angle_codes):
    return jnp.tan((angle_codes.astype(F32) - ANGLES / 2) * (math.pi / (2 * ANGLES)))


def halves(matrix):
    high = matrix.astype(ml_dtypes.bfloat16)
    low = (matrix - high.astype(np.float64)).astype(ml_dtypes.bfloat16)
    return high, low


def direct_matrices(n):
    m = np.arange(n)
    f = np.arange(n // 2)
    theta = 2 * np.pi * ((m[:, None] * f[None, :]) % n) / n
    cosines, sines = np.cos(theta), np.sin(theta)
    sines[:, 0] = (-1.0) ** m
    weight = np.full(n // 2, 2.0 / n)
    weight[0] = 1.0 / n
    forward = np.concatenate([cosines, sines], 1)
    inverse = np.concatenate([cosines * weight, sines * weight], 1).T
    return forward, inverse


def split_matrices(n):
    half = n // 2
    m = np.arange(half)
    j = np.arange(half // 2)
    out = []
    for odd in (0, 1):
        theta = 2 * np.pi * (((2 * j + odd)[:, None] * m[None, :]) % n) / n
        cosines, sines = np.cos(theta), np.sin(theta)
        weight = np.full((half // 2, 1), 2.0 / n)
        if not odd:
            sines[0] = (-1.0) ** m
            weight[0] = 1.0 / n
        out.append(np.concatenate([cosines, sines], 0))
        out.append(np.concatenate([cosines * weight, sines * weight], 0).T)
    return out


def frequencies_split(n):
    j = np.arange(n // 4)
    even = 2 * j
    even[0] = n // 2
    return np.concatenate([even, 2 * j + 1]).astype(np.float32)


def lhs3(matrix):
    high, low = halves(matrix)
    return jnp.asarray(np.concatenate([high, high, low], 1))


def rhs3(matrix):
    high, low = halves(matrix)
    return jnp.asarray(np.concatenate([high, high, low], 0))


def split(value):
    high = value.astype(BF16)
    low = (value - high.astype(F32)).astype(BF16)
    return high, low


def turn(c, s, c1, s1, c2, s2, first):
    cp = c1 * c2 - s1 * s2
    sp = s1 * c2 + c1 * s2
    cpc = cp
    if first is not None:
        cpc = jnp.where(first, 1.0, cp)
        sp = jnp.where(first, 0.0, sp)
    return c * cpc + s * sp, s * cp - c * sp


def dot(a, b):
    return jnp.dot(a, b, preferred_element_type=F32)


def turns(frequency, offsets, n):
    u = frequency * offsets * (1.0 / n)
    p = (u - jnp.round(u)) * (2.0 * math.pi)
    return jnp.cos(p), jnp.sin(p)


def iota(shape, dim):
    return lax.broadcasted_iota(jnp.int32, shape, dim)


def third_kernel(x0, size, full, place, slopes, v_ref, fw_ref, iv_ref, own_ref, other_ref, c1_scr, s1_scr, c2_scr, s2_scr):
    xb, ny, n = v_ref.shape
    half = n // 2
    step = pl.program_id(0)

    @pl.when(step == 0)
    def _():
        def offsets(count, start, total, slope):
            return slope * ((iota((count, half), 0) + start).astype(F32) - total / 2)

        def frequency(count):
            f = iota((count, half), 1)
            return jnp.where(f == 0, half, f).astype(F32)

        padded = c1_scr.shape[0]
        c1_scr[...], s1_scr[...] = turns(
            frequency(padded), offsets(padded, place[1] + x0, full[0], slopes[2, 0]), n
        )
        c2_scr[...], s2_scr[...] = turns(frequency(ny), offsets(ny, place[2] * ny, full[1], slopes[2, 1]), n)

    first = iota((ny, half), 1) == 0
    mine = place[2] == 0
    for x in range(xb):
        high, low = split(v_ref[x])
        spectrum = dot(jnp.concatenate([high, low, high], 1), fw_ref[...])
        at = pl.ds(step * xb + x, 1)
        c, s = turn(
            spectrum[:, :half], spectrum[:, half:], c1_scr[at, :], s1_scr[at, :], c2_scr[...], s2_scr[...], first
        )
        high, low = split(jnp.concatenate([c, s], 1))
        back = dot(jnp.concatenate([high, low, high], 1), iv_ref[...])
        lower, upper = back[:, :half], back[:, half:]
        own_ref[x] = jnp.where(mine, lower, upper)
        other_ref[x] = jnp.where(mine, upper, lower)


def second_kernel(
    x0, heights, part, full, place, slopes, own_ref, other_ref, fe_ref, fo_ref, ie_ref, io_ref, *rest
):
    if heights:
        outs, (c1_scr, s1_scr, c2_scr, s2_scr, p_scr, q_scr) = rest[:-6], rest[-6:]
    else:
        (out,), (c1_scr, s1_scr, c2_scr, s2_scr) = rest[:-4], rest[-4:]
    xb, half, nk = own_ref.shape
    n = 2 * half
    quarter = half // 2
    blocks = half // part
    step = pl.program_id(0)

    @pl.when(step == 0)
    def _():
        def frequency(width):
            r = iota((half, width), 0)
            f = jnp.where(r < quarter, 2 * r, 2 * (r - quarter) + 1)
            return jnp.where(r == 0, half, f).astype(F32)

        lanes = iota((half, 128), 1)
        c1, s1 = turns(frequency(128), slopes[1, 0] * ((lanes + (place[1] + x0)).astype(F32) - full[0] / 2), n)
        for b in range(c1_scr.shape[0]):
            c1_scr[b] = c1[:, b * xb : (b + 1) * xb]
            s1_scr[b] = s1[:, b * xb : (b + 1) * xb]
        lanes = iota((half, nk), 1)
        c2_scr[...], s2_scr[...] = turns(
            frequency(nk), slopes[1, 1] * ((lanes + place[2] * nk).astype(F32) - full[2] / 2), n
        )

    col_sign = (1 - 2 * place[2]).astype(F32)
    row_sign = (1 - 2 * place[3]).astype(F32)
    first = iota((quarter, nk), 0) == 0
    for x0 in range(0, xb, 2):
        pair = (x0, x0 + 1)
        total = jnp.concatenate([own_ref[x] + other_ref[x] for x in pair], 1)
        delta = jnp.concatenate([own_ref[x] - other_ref[x] for x in pair], 1) * col_sign
        results = []
        for odd, (value, fw, iv) in enumerate(((total, fe_ref, ie_ref), (delta, fo_ref, io_ref))):
            high, low = split(value)
            spectrum = dot(fw[...], jnp.concatenate([high, low, high], 0))
            frows = slice(odd * quarter, (odd + 1) * quarter)
            c2, s2 = c2_scr[frows], s2_scr[frows]
            turned = []
            for k, x in enumerate(pair):
                lanes = slice(k * nk, (k + 1) * nk)
                c, s = turn(
                    spectrum[:quarter, lanes], spectrum[quarter:, lanes],
                    c1_scr[step, frows, x : x + 1], s1_scr[step, frows, x : x + 1], c2, s2,
                    None if odd else first,
                )
                turned.append(jnp.concatenate([c, s], 0))
            high, low = split(jnp.concatenate(turned, 1))
            results.append(dot(iv[...], jnp.concatenate([high, low, high], 0)))
        p, q = results
        if not heights:
            for base, value in ((0, p + q), (blocks, p - q)):
                for j in range(blocks):
                    for k, x in enumerate(pair):
                        out[base + j, x] = value[j * part : (j + 1) * part, k * nk : (k + 1) * nk]
            continue
        q = q * row_sign
        for j in range(blocks):
            p_scr[j] = p[j * part : (j + 1) * part]
            q_scr[j] = q[j * part : (j + 1) * part]
        for j in range(blocks):
            source = lax.bitwise_xor(place[0], j)
            p, q = p_scr[source], q_scr[source]
            for slot, value in ((j, p + q), (j + blocks, p - q)):
                y = 0
                for c, height in enumerate(heights):
                    for k, x in enumerate(pair):
                        outs[slot * len(heights) + c][x] = value[y : y + height, k * nk : (k + 1) * nk]
                    y += height


def first_kernel(place, slopes, head_ref, *refs):
    slots = head_ref.shape[0]
    blocks = slots // 2
    ins, rest = refs[:slots], refs[slots:]
    fe_ref, fo_ref, ie_ref, io_ref, c1_ref, s1_ref, c2_ref, s2_ref = rest[:8]
    out_ref, token_ref, e_scr, o_scr = rest[-4:]
    token_ref[...] = jnp.zeros_like(token_ref)
    n, ny, nk = out_ref.shape
    half, quarter = n // 2, n // 4
    heads, tails = head_ref.shape[1], ins[0].shape[0]
    row_sign = (1 - 2 * place[3]).astype(F32)
    first = iota((quarter, nk), 0) == 0
    aligned = ny % 8 == 0

    def flatten(ref):
        return ref.reshape(math.prod(ref.shape[:-1]), nk) if aligned else ref

    flat_head, flat, out_flat = flatten(head_ref), [flatten(ref) for ref in ins], flatten(out_ref)

    def head(side, y):
        if aligned:
            return flat_head[pl.ds(side * blocks * heads * ny + y, blocks * heads, stride=ny), :]
        return head_ref[side * blocks : (side + 1) * blocks, :, y, :].reshape(blocks * heads, nk)

    def column(slot, y):
        if aligned:
            return flat[slot][pl.ds(y, tails, stride=ny), :]
        return ins[slot][:, y, :]

    def keep(scr, at, count, value):
        high, low = split(value)
        for k, part in enumerate((high, low, high)):
            start = at + k * half
            if not isinstance(start, int):
                start = pl.multiple_of(start, 8)
            scr[pl.ds(start, count), :] = part

    for y0 in range(0, ny, 2):
        pair = (y0, y0 + 1)
        near = jnp.concatenate([head(0, y) for y in pair], 1)
        far = jnp.concatenate([head(1, y) for y in pair], 1)
        keep(e_scr, 0, blocks * heads, near + far)
        keep(o_scr, 0, blocks * heads, near - far)
        for j in range(blocks):
            at = lax.bitwise_xor(place[0], j) * tails + blocks * heads
            near = jnp.concatenate([column(j, y) for y in pair], 1)
            far = jnp.concatenate([column(j + blocks, y) for y in pair], 1)
            keep(e_scr, at, tails, near + far)
            keep(o_scr, at, tails, (near - far) * row_sign)
        results = []
        for odd, (scr, fw, iv) in enumerate(((e_scr, fe_ref, ie_ref), (o_scr, fo_ref, io_ref))):
            spectrum = dot(fw[...], scr[...])
            frows = slice(odd * quarter, (odd + 1) * quarter)
            c2, s2 = c2_ref[frows], s2_ref[frows]
            turned = []
            for k, y in enumerate(pair):
                lanes = slice(k * nk, (k + 1) * nk)
                c, s = turn(
                    spectrum[:quarter, lanes], spectrum[quarter:, lanes],
                    c1_ref[0, frows, y : y + 1], s1_ref[0, frows, y : y + 1], c2, s2,
                    None if odd else first,
                )
                turned.append(jnp.concatenate([c, s], 0))
            high, low = split(jnp.concatenate(turned, 1))
            results.append(dot(iv[...], jnp.concatenate([high, low, high], 0)))
        p, q = results
        for at, value in ((0, p + q), (half, p - q)):
            for k, y in enumerate(pair):
                column_out = value[:, k * nk : (k + 1) * nk]
                if aligned:
                    out_flat[pl.ds(at * ny + y, half, stride=ny), :] = column_out
                else:
                    out_ref[at : at + half, y, :] = column_out


def whole(array):
    rank = array.ndim
    return pl.BlockSpec(array.shape, lambda i, *_: (0,) * rank)


def call(kernel, grid, in_specs, out_specs, out_shape, scratch, flops, moved, aliases=None, name=None):
    return pl.pallas_call(
        kernel,
        out_shape=out_shape,
        grid_spec=pltpu.PrefetchScalarGridSpec(
            num_scalar_prefetch=2, grid=(grid,), in_specs=in_specs, out_specs=out_specs, scratch_shapes=scratch
        ),
        input_output_aliases=aliases or {},
        compiler_params=pltpu.CompilerParams(vmem_limit_bytes=VMEM_LIMIT),
        cost_estimate=pl.CostEstimate(flops=1, bytes_accessed=1, transcendentals=0),
        name=name,
    )


def body(upstream, angle_codes):
    factors = shear_factors_of(angle_codes)
    row_count, col_count = lax.axis_size("row"), lax.axis_size("col")
    row_place, col_place = lax.axis_index("row"), lax.axis_index("col")
    xl, yl, nz = upstream.shape
    nx, ny = xl * row_count, yl * col_count
    full = (nx, ny, nz)
    nk, part = nz // col_count, ny // row_count
    blocks = row_count // 2
    xb = XB
    head_x = xl * HEAD // 8 if xl >= 64 else xl // 2
    tail_x = xl - head_x
    heights = tuple(part * sixths // 6 for sixths in CHUNKS) if part % 48 == 0 else (part,)
    rows = 8 if part % 8 == 0 else part
    place = jnp.stack([row_place % blocks, row_place * xl, col_place, row_place // blocks]).astype(jnp.int32)
    slopes = factors

    z_forward, z_inverse = (rhs3(matrix) for matrix in direct_matrices(nz))
    y_mats = [lhs3(matrix) for matrix in split_matrices(ny)]
    y_mats = [y_mats[0], y_mats[2], y_mats[1], y_mats[3]]
    places = np.arange(nx // 2).reshape(blocks, xl)
    arrival = np.concatenate([places[:, :head_x].reshape(-1), places[:, head_x:].reshape(-1)])
    x_even, x_even_back, x_odd, x_odd_back = split_matrices(nx)
    x_mats = [lhs3(matrix) for matrix in (x_even[:, arrival], x_odd[:, arrival], x_even_back, x_odd_back)]

    def third(x0, size, volume):
        base = x0 // xb
        out = pl.BlockSpec((xb, yl, nk), lambda i, *_: (i, 0, 0))
        near = pltpu.VMEM((-(-size // 8) * 8, nz // 2), F32)
        far = pltpu.VMEM((yl, nz // 2), F32)
        return call(
            functools.partial(third_kernel, x0, size, full), size // xb,
            [pl.BlockSpec((xb, yl, nz), lambda i, *_: (base + i, 0, 0)), whole(z_forward), whole(z_inverse)],
            [out, out],
            [jax.ShapeDtypeStruct((size, yl, nk), F32)] * 2,
            [near, near, far, far], 12 * size * yl * nz * nz, 8 * size * yl * nz, name="third",
        )(place, slopes, volume, z_forward, z_inverse)

    def second(x0, size, own, other, heights):
        data = pl.BlockSpec((xb, yl, nk), lambda i, *_: (i, 0, 0))
        near = pltpu.VMEM((size // xb, ny // 2, xb), F32)
        far = pltpu.VMEM((ny // 2, nk), F32)
        scratch = [near, near, far, far]
        if heights:
            scratch += [pltpu.VMEM((blocks, part, 2 * nk), F32)] * 2
            specs = [pl.BlockSpec((xb, height, nk), lambda i, *_: (i, 0, 0)) for height in heights] * row_count
            shapes = [jax.ShapeDtypeStruct((size, height, nk), F32) for height in heights] * row_count
        else:
            specs = [pl.BlockSpec((row_count, xb, part, nk), lambda i, *_: (0, i, 0, 0))]
            shapes = [jax.ShapeDtypeStruct((row_count, size, part, nk), F32)]
        return call(
            functools.partial(second_kernel, x0, heights, part, full), size // xb,
            [data, data] + [whole(matrix) for matrix in y_mats],
            specs, shapes, scratch, 6 * size * ny * nk * ny, 8 * size * ny * nk, name="second",
        )(place, slopes, own, other, *y_mats)

    sent = []
    order = [d for pair in zip([*range(1, blocks), 0], range(blocks, row_count)) for d in pair if d]

    def after(value, *others):
        return lax.optimization_barrier((value, *others))[0]

    def spread(pieces, order, gates=None):
        got = [pieces[0]] + [None] * (row_count - 1)
        for i, d in enumerate(order):
            others = list(sent[-WINDOW:][:1]) if len(sent) >= WINDOW else []
            if gates and i in gates:
                others.append(gates[i])
            got[d] = lax.ppermute(after(pieces[d], *others), "row", [(i, i ^ d) for i in range(row_count)])
            sent.append(got[d])
        return got

    swap = [(0, 1), (1, 0)]
    own, other = third(0, head_x, upstream)
    (head,) = second(0, head_x, own, lax.ppermute(other, "col", swap), None)
    volume = after(upstream, head)
    head = lax.all_to_all(head, "row", 0, 0, tiled=True)
    own, other = third(head_x, tail_x, volume)
    outs = second(head_x, tail_x, own, lax.ppermute(other, "col", swap), heights)
    pieces = [[outs[d * len(heights) + c] for d in range(row_count)] for c in range(len(heights))]

    def waves(frequency, offsets, n):
        p = frequency * offsets * (2.0 * math.pi / n)
        return jnp.cos(p), jnp.sin(p)

    def centred(length, start, total):
        return (lax.iota(jnp.int32, length) + start).astype(F32) - total / 2

    late = after(slopes, outs[0])
    fx = frequencies_split(nx)
    xc1, xs1 = waves(fx[None, :, None], (late[0, 0] * centred(part, row_place * part, ny)).reshape(-1, 1, rows), nx)
    xc2, xs2 = waves(fx[:, None], (late[0, 1] * centred(nk, col_place * nk, nz))[None, :], nx)

    def first(y0, height, got, result, token):
        base = y0 // rows
        ins = [head, *got]
        specs = [pl.BlockSpec((row_count, head_x, rows, nk), lambda i, *_: (0, 0, base + i, 0))]
        specs += [pl.BlockSpec((tail_x, rows, nk), lambda i, *_: (0, i, 0))] * row_count
        table = pl.BlockSpec((1, nx // 2, rows), lambda i, *_: (base + i, 0, 0))
        ins += [*x_mats, xc1, xs1, xc2, xs2]
        specs += [whole(matrix) for matrix in x_mats] + [table, table, whole(xc2), whole(xs2)]
        aliases = {}
        if result is not None:
            aliases = {len(ins) + 2: 0}
            ins += [result, token]
            specs += [pl.BlockSpec(memory_space=pl.ANY)] * 2
        scratch = pltpu.VMEM((3 * nx // 2, 2 * nk), BF16)
        return call(
            first_kernel, height // rows,
            specs,
            [pl.BlockSpec((nx, rows, nk), lambda i, *_: (0, base + i, 0)), pl.BlockSpec((8, 128), lambda i, *_: (0, 0))],
            [jax.ShapeDtypeStruct((nx, part, nk), F32), jax.ShapeDtypeStruct((8, 128), F32)],
            [scratch, scratch], 6 * nx * height * nk * nx, 8 * nx * height * nk, aliases, name="first",
        )(place, slopes, *ins)

    result, token, tokens, y0 = None, None, [], 0
    last = [*order[:-3], *order[-3:-1][::-1], order[-1]]
    got = [spread(pieces[0], order, {i: head for i in GATES})]
    for c, height in enumerate(heights):
        ahead = c + 1
        if ahead < len(heights):
            gates = {}
            if c >= 1:
                gates[0] = tokens[c - 1]
            if ahead == len(heights) - 1 and c >= 1:
                result, token = first(y0, height, got[c], result, token)
                tokens.append(token)
                gates[len(order) - 2] = token
            got.append(spread(pieces[ahead], last if ahead == len(heights) - 1 else order, gates))
        if len(tokens) == c:
            result, token = first(y0, height, got[c], result, token)
            tokens.append(token)
        y0 += height
    return result


def solution(mesh):
    placed = (P(("grp", "row"), "col", None), P("grp", None))
    return jax.shard_map(
        body, mesh=mesh, in_specs=placed, out_specs=P("grp", "row", "col"), check_vma=False
    )
```

```python
import functools
import math

import jax
import jax.numpy as jnp
import ml_dtypes
import numpy as np
from jax import lax
from jax.experimental import pallas as pl
from jax.experimental.pallas import tpu as pltpu
from jax.sharding import PartitionSpec as P

ANGLES = 360
F32 = jnp.float32
BF16 = jnp.bfloat16
VMEM_LIMIT = 58 * 1024 * 1024
XB = 8
HEAD = 2
CHUNKS = (3, 2, 1)
GATES = (3,)
WINDOW = 5


def shear_factors_of(angle_codes):
    return jnp.tan((angle_codes.astype(F32) - ANGLES / 2) * (math.pi / (2 * ANGLES)))


def halves(matrix):
    high = matrix.astype(ml_dtypes.bfloat16)
    low = (matrix - high.astype(np.float64)).astype(ml_dtypes.bfloat16)
    return high, low


def direct_matrices(n):
    m = np.arange(n)
    f = np.arange(n // 2)
    theta = 2 * np.pi * ((m[:, None] * f[None, :]) % n) / n
    cosines, sines = np.cos(theta), np.sin(theta)
    sines[:, 0] = (-1.0) ** m
    weight = np.full(n // 2, 2.0 / n)
    weight[0] = 1.0 / n
    forward = np.concatenate([cosines, sines], 1)
    inverse = np.concatenate([cosines * weight, sines * weight], 1).T
    return forward, inverse


def split_matrices(n):
    half = n // 2
    m = np.arange(half)
    j = np.arange(half // 2)
    out = []
    for odd in (0, 1):
        theta = 2 * np.pi * (((2 * j + odd)[:, None] * m[None, :]) % n) / n
        cosines, sines = np.cos(theta), np.sin(theta)
        weight = np.full((half // 2, 1), 2.0 / n)
        if not odd:
            sines[0] = (-1.0) ** m
            weight[0] = 1.0 / n
        out.append(np.concatenate([cosines, sines], 0))
        out.append(np.concatenate([cosines * weight, sines * weight], 0).T)
    return out


def frequencies_split(n):
    j = np.arange(n // 4)
    even = 2 * j
    even[0] = n // 2
    return np.concatenate([even, 2 * j + 1]).astype(np.float32)


def lhs3(matrix):
    high, low = halves(matrix)
    return jnp.asarray(np.concatenate([high, high, low], 1))


def rhs3(matrix):
    high, low = halves(matrix)
    return jnp.asarray(np.concatenate([high, high, low], 0))


def split(value):
    high = value.astype(BF16)
    low = (value - high.astype(F32)).astype(BF16)
    return high, low


def turn(c, s, c1, s1, c2, s2, first):
    cp = c1 * c2 - s1 * s2
    sp = s1 * c2 + c1 * s2
    cpc = cp
    if first is not None:
        cpc = jnp.where(first, 1.0, cp)
        sp = jnp.where(first, 0.0, sp)
    return c * cpc + s * sp, s * cp - c * sp


def dot(a, b):
    return jnp.dot(a, b, preferred_element_type=F32)


def turns(frequency, offsets, n):
    u = frequency * offsets * (1.0 / n)
    p = (u - jnp.round(u)) * (2.0 * math.pi)
    return jnp.cos(p), jnp.sin(p)


def iota(shape, dim):
    return lax.broadcasted_iota(jnp.int32, shape, dim)


def third_kernel(x0, size, full, place, slopes, v_ref, fw_ref, iv_ref, own_ref, other_ref, c1_scr, s1_scr, c2_scr, s2_scr):
    xb, ny, n = v_ref.shape
    half = n // 2
    step = pl.program_id(0)

    @pl.when(step == 0)
    def _():
        def offsets(count, start, total, slope):
            return slope * ((iota((count, half), 0) + start).astype(F32) - total / 2)

        def frequency(count):
            f = iota((count, half), 1)
            return jnp.where(f == 0, half, f).astype(F32)

        padded = c1_scr.shape[0]
        c1_scr[...], s1_scr[...] = turns(
            frequency(padded), offsets(padded, place[1] + x0, full[0], slopes[2, 0]), n
        )
        c2_scr[...], s2_scr[...] = turns(frequency(ny), offsets(ny, place[2] * ny, full[1], slopes[2, 1]), n)

    first = iota((ny, half), 1) == 0
    mine = place[2] == 0
    for x in range(xb):
        high, low = split(v_ref[x])
        spectrum = dot(jnp.concatenate([high, low, high], 1), fw_ref[...])
        at = pl.ds(step * xb + x, 1)
        c, s = turn(
            spectrum[:, :half], spectrum[:, half:], c1_scr[at, :], s1_scr[at, :], c2_scr[...], s2_scr[...], first
        )
        high, low = split(jnp.concatenate([c, s], 1))
        back = dot(jnp.concatenate([high, low, high], 1), iv_ref[...])
        lower, upper = back[:, :half], back[:, half:]
        own_ref[x] = jnp.where(mine, lower, upper)
        other_ref[x] = jnp.where(mine, upper, lower)


def second_kernel(
    x0, heights, part, full, place, slopes, own_ref, other_ref, fe_ref, fo_ref, ie_ref, io_ref, *rest
):
    if heights:
        outs, (c1_scr, s1_scr, c2_scr, s2_scr, p_scr, q_scr) = rest[:-6], rest[-6:]
    else:
        (out,), (c1_scr, s1_scr, c2_scr, s2_scr) = rest[:-4], rest[-4:]
    xb, half, nk = own_ref.shape
    n = 2 * half
    quarter = half // 2
    blocks = half // part
    step = pl.program_id(0)

    @pl.when(step == 0)
    def _():
        def frequency(width):
            r = iota((half, width), 0)
            f = jnp.where(r < quarter, 2 * r, 2 * (r - quarter) + 1)
            return jnp.where(r == 0, half, f).astype(F32)

        lanes = iota((half, 128), 1)
        c1, s1 = turns(frequency(128), slopes[1, 0] * ((lanes + (place[1] + x0)).astype(F32) - full[0] / 2), n)
        for b in range(c1_scr.shape[0]):
            c1_scr[b] = c1[:, b * xb : (b + 1) * xb]
            s1_scr[b] = s1[:, b * xb : (b + 1) * xb]
        lanes = iota((half, nk), 1)
        c2_scr[...], s2_scr[...] = turns(
            frequency(nk), slopes[1, 1] * ((lanes + place[2] * nk).astype(F32) - full[2] / 2), n
        )

    col_sign = (1 - 2 * place[2]).astype(F32)
    row_sign = (1 - 2 * place[3]).astype(F32)
    first = iota((quarter, nk), 0) == 0
    for x0 in range(0, xb, 2):
        pair = (x0, x0 + 1)
        total = jnp.concatenate([own_ref[x] + other_ref[x] for x in pair], 1)
        delta = jnp.concatenate([own_ref[x] - other_ref[x] for x in pair], 1) * col_sign
        results = []
        for odd, (value, fw, iv) in enumerate(((total, fe_ref, ie_ref), (delta, fo_ref, io_ref))):
            high, low = split(value)
            spectrum = dot(fw[...], jnp.concatenate([high, low, high], 0))
            frows = slice(odd * quarter, (odd + 1) * quarter)
            c2, s2 = c2_scr[frows], s2_scr[frows]
            turned = []
            for k, x in enumerate(pair):
                lanes = slice(k * nk, (k + 1) * nk)
                c, s = turn(
                    spectrum[:quarter, lanes], spectrum[quarter:, lanes],
                    c1_scr[step, frows, x : x + 1], s1_scr[step, frows, x : x + 1], c2, s2,
                    None if odd else first,
                )
                turned.append(jnp.concatenate([c, s], 0))
            high, low = split(jnp.concatenate(turned, 1))
            results.append(dot(iv[...], jnp.concatenate([high, low, high], 0)))
        p, q = results
        if not heights:
            for base, value in ((0, p + q), (blocks, p - q)):
                for j in range(blocks):
                    for k, x in enumerate(pair):
                        out[base + j, x] = value[j * part : (j + 1) * part, k * nk : (k + 1) * nk]
            continue
        q = q * row_sign
        for j in range(blocks):
            p_scr[j] = p[j * part : (j + 1) * part]
            q_scr[j] = q[j * part : (j + 1) * part]
        for j in range(blocks):
            source = lax.bitwise_xor(place[0], j)
            p, q = p_scr[source], q_scr[source]
            for slot, value in ((j, p + q), (j + blocks, p - q)):
                y = 0
                for c, height in enumerate(heights):
                    for k, x in enumerate(pair):
                        outs[slot * len(heights) + c][x] = value[y : y + height, k * nk : (k + 1) * nk]
                    y += height


def first_kernel(place, slopes, head_ref, *refs):
    slots = head_ref.shape[0]
    blocks = slots // 2
    ins, rest = refs[:slots], refs[slots:]
    fe_ref, fo_ref, ie_ref, io_ref, c1_ref, s1_ref, c2_ref, s2_ref = rest[:8]
    out_ref, token_ref, e_scr, o_scr = rest[-4:]
    token_ref[...] = jnp.zeros_like(token_ref)
    n, ny, nk = out_ref.shape
    half, quarter = n // 2, n // 4
    heads, tails = head_ref.shape[1], ins[0].shape[0]
    row_sign = (1 - 2 * place[3]).astype(F32)
    first = iota((quarter, nk), 0) == 0
    aligned = ny % 8 == 0

    def flatten(ref):
        return ref.reshape(math.prod(ref.shape[:-1]), nk) if aligned else ref

    flat_head, flat, out_flat = flatten(head_ref), [flatten(ref) for ref in ins], flatten(out_ref)

    def head(side, y):
        if aligned:
            return flat_head[pl.ds(side * blocks * heads * ny + y, blocks * heads, stride=ny), :]
        return head_ref[side * blocks : (side + 1) * blocks, :, y, :].reshape(blocks * heads, nk)

    def column(slot, y):
        if aligned:
            return flat[slot][pl.ds(y, tails, stride=ny), :]
        return ins[slot][:, y, :]

    def keep(scr, at, count, value):
        high, low = split(value)
        for k, part in enumerate((high, low, high)):
            start = at + k * half
            if not isinstance(start, int):
                start = pl.multiple_of(start, 8)
            scr[pl.ds(start, count), :] = part

    for y0 in range(0, ny, 2):
        pair = (y0, y0 + 1)
        near = jnp.concatenate([head(0, y) for y in pair], 1)
        far = jnp.concatenate([head(1, y) for y in pair], 1)
        keep(e_scr, 0, blocks * heads, near + far)
        keep(o_scr, 0, blocks * heads, near - far)
        for j in range(blocks):
            at = lax.bitwise_xor(place[0], j) * tails + blocks * heads
            near = jnp.concatenate([column(j, y) for y in pair], 1)
            far = jnp.concatenate([column(j + blocks, y) for y in pair], 1)
            keep(e_scr, at, tails, near + far)
            keep(o_scr, at, tails, (near - far) * row_sign)
        results = []
        for odd, (scr, fw, iv) in enumerate(((e_scr, fe_ref, ie_ref), (o_scr, fo_ref, io_ref))):
            spectrum = dot(fw[...], scr[...])
            frows = slice(odd * quarter, (odd + 1) * quarter)
            c2, s2 = c2_ref[frows], s2_ref[frows]
            turned = []
            for k, y in enumerate(pair):
                lanes = slice(k * nk, (k + 1) * nk)
                c, s = turn(
                    spectrum[:quarter, lanes], spectrum[quarter:, lanes],
                    c1_ref[0, frows, y : y + 1], s1_ref[0, frows, y : y + 1], c2, s2,
                    None if odd else first,
                )
                turned.append(jnp.concatenate([c, s], 0))
            high, low = split(jnp.concatenate(turned, 1))
            results.append(dot(iv[...], jnp.concatenate([high, low, high], 0)))
        p, q = results
        for at, value in ((0, p + q), (half, p - q)):
            for k, y in enumerate(pair):
                column_out = value[:, k * nk : (k + 1) * nk]
                if aligned:
                    out_flat[pl.ds(at * ny + y, half, stride=ny), :] = column_out
                else:
                    out_ref[at : at + half, y, :] = column_out


def whole(array):
    rank = array.ndim
    return pl.BlockSpec(array.shape, lambda i, *_: (0,) * rank)


def call(kernel, grid, in_specs, out_specs, out_shape, scratch, flops, moved, aliases=None, name=None):
    return pl.pallas_call(
        kernel,
        out_shape=out_shape,
        grid_spec=pltpu.PrefetchScalarGridSpec(
            num_scalar_prefetch=2, grid=(grid,), in_specs=in_specs, out_specs=out_specs, scratch_shapes=scratch
        ),
        input_output_aliases=aliases or {},
        compiler_params=pltpu.CompilerParams(vmem_limit_bytes=VMEM_LIMIT),
        cost_estimate=pl.CostEstimate(flops=1, bytes_accessed=1, transcendentals=0),
        name=name,
    )


def body(upstream, angle_codes):
    factors = shear_factors_of(angle_codes)
    row_count, col_count = lax.axis_size("row"), lax.axis_size("col")
    row_place, col_place = lax.axis_index("row"), lax.axis_index("col")
    xl, yl, nz = upstream.shape
    nx, ny = xl * row_count, yl * col_count
    full = (nx, ny, nz)
    nk, part = nz // col_count, ny // row_count
    blocks = row_count // 2
    xb = XB
    head_x = xl * HEAD // 8 if xl >= 64 else xl // 2
    tail_x = xl - head_x
    heights = tuple(part * sixths // 6 for sixths in CHUNKS) if part % 48 == 0 else (part,)
    rows = 8 if part % 8 == 0 else part
    place = jnp.stack([row_place % blocks, row_place * xl, col_place, row_place // blocks]).astype(jnp.int32)
    slopes = factors

    z_forward, z_inverse = (rhs3(matrix) for matrix in direct_matrices(nz))
    y_mats = [lhs3(matrix) for matrix in split_matrices(ny)]
    y_mats = [y_mats[0], y_mats[2], y_mats[1], y_mats[3]]
    places = np.arange(nx // 2).reshape(blocks, xl)
    arrival = np.concatenate([places[:, :head_x].reshape(-1), places[:, head_x:].reshape(-1)])
    x_even, x_even_back, x_odd, x_odd_back = split_matrices(nx)
    x_mats = [lhs3(matrix) for matrix in (x_even[:, arrival], x_odd[:, arrival], x_even_back, x_odd_back)]

    def third(x0, size, volume):
        base = x0 // xb
        out = pl.BlockSpec((xb, yl, nk), lambda i, *_: (i, 0, 0))
        near = pltpu.VMEM((-(-size // 8) * 8, nz // 2), F32)
        far = pltpu.VMEM((yl, nz // 2), F32)
        return call(
            functools.partial(third_kernel, x0, size, full), size // xb,
            [pl.BlockSpec((xb, yl, nz), lambda i, *_: (base + i, 0, 0)), whole(z_forward), whole(z_inverse)],
            [out, out],
            [jax.ShapeDtypeStruct((size, yl, nk), F32)] * 2,
            [near, near, far, far], 12 * size * yl * nz * nz, 8 * size * yl * nz, name="third",
        )(place, slopes, volume, z_forward, z_inverse)

    def second(x0, size, own, other, heights):
        data = pl.BlockSpec((xb, yl, nk), lambda i, *_: (i, 0, 0))
        near = pltpu.VMEM((size // xb, ny // 2, xb), F32)
        far = pltpu.VMEM((ny // 2, nk), F32)
        scratch = [near, near, far, far]
        if heights:
            scratch += [pltpu.VMEM((blocks, part, 2 * nk), F32)] * 2
            specs = [pl.BlockSpec((xb, height, nk), lambda i, *_: (i, 0, 0)) for height in heights] * row_count
            shapes = [jax.ShapeDtypeStruct((size, height, nk), F32) for height in heights] * row_count
        else:
            specs = [pl.BlockSpec((row_count, xb, part, nk), lambda i, *_: (0, i, 0, 0))]
            shapes = [jax.ShapeDtypeStruct((row_count, size, part, nk), F32)]
        return call(
            functools.partial(second_kernel, x0, heights, part, full), size // xb,
            [data, data] + [whole(matrix) for matrix in y_mats],
            specs, shapes, scratch, 6 * size * ny * nk * ny, 8 * size * ny * nk, name="second",
        )(place, slopes, own, other, *y_mats)

    sent = []
    order = [d for pair in zip([*range(1, blocks), 0], range(blocks, row_count)) for d in pair if d]

    def after(value, *others):
        return lax.optimization_barrier((value, *others))[0]

    def spread(pieces, gates=None):
        got = [pieces[0]] + [None] * (row_count - 1)
        for i, d in enumerate(order):
            others = list(sent[-WINDOW:][:1]) if len(sent) >= WINDOW else []
            if gates and i in gates:
                others.append(gates[i])
            got[d] = lax.ppermute(after(pieces[d], *others), "row", [(i, i ^ d) for i in range(row_count)])
            sent.append(got[d])
        return got

    swap = [(0, 1), (1, 0)]
    own, other = third(0, head_x, upstream)
    (head,) = second(0, head_x, own, lax.ppermute(other, "col", swap), None)
    volume = after(upstream, head)
    head = lax.all_to_all(head, "row", 0, 0, tiled=True)
    own, other = third(head_x, tail_x, volume)
    outs = second(head_x, tail_x, own, lax.ppermute(other, "col", swap), heights)
    pieces = [[outs[d * len(heights) + c] for d in range(row_count)] for c in range(len(heights))]

    def waves(frequency, offsets, n):
        p = frequency * offsets * (2.0 * math.pi / n)
        return jnp.cos(p), jnp.sin(p)

    def centred(length, start, total):
        return (lax.iota(jnp.int32, length) + start).astype(F32) - total / 2

    late = after(slopes, outs[0])
    fx = frequencies_split(nx)
    xc1, xs1 = waves(fx[None, :, None], (late[0, 0] * centred(part, row_place * part, ny)).reshape(-1, 1, rows), nx)
    xc2, xs2 = waves(fx[:, None], (late[0, 1] * centred(nk, col_place * nk, nz))[None, :], nx)

    def first(y0, height, got, result, token):
        base = y0 // rows
        ins = [head, *got]
        specs = [pl.BlockSpec((row_count, head_x, rows, nk), lambda i, *_: (0, 0, base + i, 0))]
        specs += [pl.BlockSpec((tail_x, rows, nk), lambda i, *_: (0, i, 0))] * row_count
        table = pl.BlockSpec((1, nx // 2, rows), lambda i, *_: (base + i, 0, 0))
        ins += [*x_mats, xc1, xs1, xc2, xs2]
        specs += [whole(matrix) for matrix in x_mats] + [table, table, whole(xc2), whole(xs2)]
        aliases = {}
        if result is not None:
            aliases = {len(ins) + 2: 0}
            ins += [result, token]
            specs += [pl.BlockSpec(memory_space=pl.ANY)] * 2
        scratch = pltpu.VMEM((3 * nx // 2, 2 * nk), BF16)
        return call(
            first_kernel, height // rows,
            specs,
            [pl.BlockSpec((nx, rows, nk), lambda i, *_: (0, base + i, 0)), pl.BlockSpec((8, 128), lambda i, *_: (0, 0))],
            [jax.ShapeDtypeStruct((nx, part, nk), F32), jax.ShapeDtypeStruct((8, 128), F32)],
            [scratch, scratch], 6 * nx * height * nk * nx, 8 * nx * height * nk, aliases, name="first",
        )(place, slopes, *ins)

    result, token, tokens, y0 = None, None, [], 0
    got = [spread(pieces[0], {i: head for i in GATES})]
    for c, height in enumerate(heights):
        ahead = c + 1
        if ahead < len(heights):
            gates = {}
            if c >= 1:
                gates[0] = tokens[c - 1]
            if ahead == len(heights) - 1 and c >= 1:
                result, token = first(y0, height, got[c], result, token)
                tokens.append(token)
                gates[len(order) - 2] = token
            got.append(spread(pieces[ahead], gates))
        if len(tokens) == c:
            result, token = first(y0, height, got[c], result, token)
            tokens.append(token)
        y0 += height
    return result


def solution(mesh):
    placed = (P(("grp", "row"), "col", None), P("grp", None))
    return jax.shard_map(
        body, mesh=mesh, in_specs=placed, out_specs=P("grp", "row", "col"), check_vma=False
    )
```
